256 devices in a mesh: dp: 16 (over x, y), seq: 8 (over z_hi, core), mp: 2 (over z_lo).
Axes of the slice: x: 4, y: 4, z: 8 (z_hi: 4, z_lo: 2; z = z_hi * 2 + z_lo), core: 2. Of those that a mesh axis runs over, the one named last changes fastest.
Arguments:
- hidden_states: bfloat16 [8192, 2048], P(('dp', 'seq')), may hold values from -6 to 6
- embeddings: bfloat16 [8192, 2048], P(('dp', 'seq')), may hold values from -6 to 6
- norm_gain: float32 [4096], replicated, may hold values from 0.1 to 1.9
- input_weights: bfloat16 [4096, 3, 2, 2048], P('dp', None, 'mp', 'seq'), may hold values from -0.09375 to 0.09375
- adapter_down: bfloat16 [4096, 384], P(('seq', 'mp')), may hold values from -0.09375 to 0.09375
- adapter_up: bfloat16 [3, 128, 2, 2048], P(None, None, 'mp', 'seq'), may hold values from -0.5 to 0.5
- output_weights: bfloat16 [2, 2048, 2048], P('mp', 'seq', 'dp'), may hold values from -3 to 3
- own_keys: bfloat16 [16, 8192, 4096], P('dp', 'seq', 'mp'), may hold values from -164 to 164
- own_values: bfloat16 [16, 8192, 4096], P('dp', 'seq', 'mp'), may hold values from -6 to 6
- shared_keys: bfloat16 [2, 1024, 4096], P(None, 'seq', 'mp'), may hold values from -164 to 164
- shared_values: bfloat16 [2, 1024, 4096], P(None, 'seq', 'mp'), may hold values from -6 to 6
- cached_lengths: int32 [16], P('dp'), may hold values from 1 to 8192, 65536 in all
- prompt_group: int32 [16], P('dp'), may hold values from 0 to 1
- slot_pages: int32 [16, 128], P('dp', 'seq'), may hold values from 0 to 127, as said below
- padding_mask: int32 [8192], P(('dp', 'seq', 'mp')), may hold values from 0 to 1, as said below
Outputs:
- mixed: bfloat16 [8192, 2048], P(('dp', 'seq', 'mp'))
The draws below stay inside these ranges and needn't reach their ends.
Inputs may be any that keep to these rules, and one draw needn't show every extreme that they name: `slot_pages`: row r maps the 128 page slots of request r one to one onto its pages: slot u holds page (u + c * 16) mod 128 for a whole number c of request r; page p holds own positions p * 64 to p * 64 + 63. `padding_mask`: within each request's 512 tokens the ones come first, then the zeros; at least 128 ones.
All inputs are finite; a program needn't handle non-finite values. No bound on the sum of `cached_lengths` on one device may be relied on, other than what follows from the above.
Results may differ from the reference program's by a relative error of at most 0.025.
The reference program's roundings to bfloat16 on the way count: a program that leaves them out, or rounds other values in their place, can miss the bound.
Values may be sent and summed in bfloat16 or wider, within the bound.
A program may use at most 128 MiB of HBM per device.

```python
import math
import jax
import jax.numpy as jnp
import numpy as np
from jax import lax

D = 2048
HEADS = 32
HD = 128
RANK = 128
NEW = 512
PAGE = 64
NGROUPS = 2
OWN_DEV = 1024
SHARED_DEV = 128
D_IN = 4096
HEADS_MP = 16
REQS = 16
TOKENS = 8192
OWN_MAX = 8192
SHARED = 1024
PAGES = 128
PAGES_DEV = 16
N_SEQ = 8
N_MP = 2


def spiked_keys(key, shape):
    base_key = jax.random.fold_in(key, 0)
    values = jnp.clip(jax.random.normal(base_key, shape, jnp.float32), -6.0, 6.0)
    return values.astype(jnp.bfloat16)


def draw_own_keys(key, part):
    return spiked_keys(jax.random.fold_in(key, 11), (REQS, OWN_MAX, HEADS * HD))


def draw_shared_keys(key, part):
    return spiked_keys(jax.random.fold_in(key, 13), (NGROUPS, SHARED, HEADS * HD))


def draw_prompt_group(key, part):
    groups = jax.random.randint(jax.random.fold_in(key, 17), (REQS,), 0, NGROUPS)
    return groups.at[0].set(0).at[1].set(1).astype(jnp.int32)


def draw_slot_pages(key, part):
    shifts = jax.random.randint(jax.random.fold_in(key, 19), (REQS, 1), 0, PAGES // PAGES_DEV)
    pages = (jnp.arange(PAGES, dtype=jnp.int32)[None, :] + shifts * PAGES_DEV) % PAGES
    return pages.astype(jnp.int32)


def draw_padding_mask(key, part):
    counts = jax.random.randint(jax.random.fold_in(key, 23), (REQS,), NEW // 4, NEW + 1)
    counts = counts.at[0].set(NEW).at[REQS - 1].set(NEW // 2)
    places = jnp.arange(NEW, dtype=jnp.int32)
    return (places[None, :] < counts[:, None]).astype(jnp.int32).reshape(TOKENS)


def steps_of(rng, shape, shards, least, largest):
    loudness, own = 1.0, jax.random.fold_in(rng, 6)
    for position, blocks in shards:
        draws = jnp.exp(jax.random.uniform(jax.random.fold_in(own, position), (blocks,), jnp.float32, least / len(shards), largest / len(shards)))
        loudness = loudness * jnp.repeat(draws, shape[position] // blocks).reshape([-1 if axis == position else 1 for axis in range(len(shape))])
    return loudness


def profile(count, total, reach, lean):
    weights = [(1 << 20) // math.isqrt(rank ** lean) + 1 for rank in range(2, count + 1)]
    surplus, given = total - reach - (count - 1), [1] * (count - 1)
    while surplus > 0:
        free = [i for i in range(count - 1) if given[i] < reach]
        mass, remaining = sum([weights[i] for i in free]), surplus
        for i in free:
            addition = min(reach - given[i], max(1, remaining * weights[i] // mass), surplus)
            given[i] = given[i] + addition
            surplus = surplus - addition
    return np.array([reach] + given)


def ragged(own_key, count, total, limit, skew):
    if count == 2:
        one = jax.random.randint(own_key, (), max(1, total - limit), min(limit, total - 1) + 1)
        return jnp.stack([one, total - one])
    lengths = jnp.asarray(profile(count, total, limit, skew), jnp.int32)
    couples = (count - 1) // 2
    giver, receiver = lengths[1:1 + 2 * couples:2], lengths[2:2 + 2 * couples:2]
    room = jnp.minimum(giver - 1, limit - receiver)
    passed = jax.random.randint(jax.random.fold_in(own_key, 1), (couples,), 0, 1 << 20) % (room + 1)
    lengths = lengths.at[1:1 + 2 * couples:2].set(giver - passed).at[2:2 + 2 * couples:2].set(receiver + passed)
    return lengths[jax.random.permutation(jax.random.fold_in(own_key, 2), count)]


def bell_draw(rng, shape, width, reach, shards=(), kind=jnp.bfloat16):
    level = steps_of(rng, shape, shards, -0.22, 0.18) if shards else 1.0
    values = jax.random.normal(rng, shape, jnp.float32) * width * level
    return jnp.minimum(jnp.maximum(values, -reach), reach).astype(kind)


def setup_inputs(seed: int = 0) -> dict:
    streams_of = jax.random.split(jax.random.key(seed), 16)
    return {
        "hidden_states": bell_draw(streams_of[0], (TOKENS, D), 1.0, 6.0, ((0, 128),)),
        "embeddings": bell_draw(streams_of[1], (TOKENS, D), 1.0, 6.0, ((0, 128),)),
        "norm_gain": jnp.clip(1.0 + 0.18 * jax.random.normal(streams_of[2], (D_IN,), jnp.float32), 0.1, 1.9),
        "input_weights": bell_draw(streams_of[3], (D_IN, 3, N_MP, HEADS_MP * HD), D_IN ** -0.5, 0.09375, ((0, 16), (2, 2), (3, 8))),
        "adapter_down": bell_draw(streams_of[4], (D_IN, 3 * RANK), D_IN ** -0.5, 0.09375, ((0, 16),)),
        "adapter_up": bell_draw(streams_of[5], (3, RANK, N_MP, HEADS_MP * HD), RANK ** -0.5, 0.5, ((2, 2), (3, 8))),
        "output_weights": bell_draw(streams_of[6], (N_MP, HEADS_MP * HD, D), (12 / (HEADS * HD) ** 0.5), 3.0, ((0, 2), (1, 8), (2, 16))),
        "own_keys": draw_own_keys(jax.random.fold_in(streams_of[15], 71), 0),
        "own_values": bell_draw(streams_of[8], (REQS, OWN_MAX, HEADS * HD), 1.0, 6.0, ((0, 16), (1, 8), (2, 2))),
        "shared_keys": draw_shared_keys(jax.random.fold_in(streams_of[15], 71), 0),
        "shared_values": bell_draw(streams_of[10], (NGROUPS, SHARED, HEADS * HD), 1.0, 6.0, ((1, 8), (2, 2))),
        "cached_lengths": ragged(streams_of[11], REQS, REQS * OWN_MAX // 2, OWN_MAX, 2).astype(jnp.int32),
        "prompt_group": draw_prompt_group(jax.random.fold_in(streams_of[15], 71), 0),
        "slot_pages": draw_slot_pages(jax.random.fold_in(streams_of[15], 71), 0),
        "padding_mask": draw_padding_mask(jax.random.fold_in(streams_of[15], 71), 0),
    }


eps = 1e-05
neg_fill = -1e+30

def to_narrow(values):
    return lax.optimization_barrier(values.astype(jnp.bfloat16))

def normalize(hidden_rows, embed_rows, norm_gain):
    joined = jnp.concatenate([hidden_rows, embed_rows], axis=1).astype(jnp.float32)
    factor = lax.rsqrt(lax.optimization_barrier(jnp.mean(joined * joined, axis=1, keepdims=True)) + eps)
    return to_narrow(joined * factor * norm_gain)

def block_partial(queries, keys, values, usable):
    scaling = 1.0 / math.sqrt(queries.shape[2])
    scores = jnp.einsum('ihd,jhd->hij', queries.astype(jnp.float32), keys.astype(jnp.float32)) * scaling
    scores = jnp.where(usable[None], scores, neg_fill)
    peak_score = lax.optimization_barrier(jnp.max(scores, axis=2))
    exponent = jnp.exp(scores - peak_score[:, :, None])
    totals = lax.optimization_barrier(jnp.sum(exponent, axis=2))
    narrow = to_narrow(exponent)
    weighted = jnp.einsum('hij,jhd->ihd', narrow.astype(jnp.float32), values.astype(jnp.float32))
    weighted = weighted / jnp.transpose(totals)[:, :, None]
    return (to_narrow(weighted), jnp.transpose(peak_score), jnp.transpose(totals))

def fold_partials(outputs, peak_scores, totals):
    highest = lax.optimization_barrier(jnp.max(peak_scores, axis=0))
    weight = totals * jnp.exp(peak_scores - highest)
    return lax.optimization_barrier(jnp.sum(weight[..., None] * outputs, axis=0)) / lax.optimization_barrier(jnp.sum(weight, axis=0))[..., None]

def reference(hidden_states, embeddings, norm_gain, input_weights, adapter_down, adapter_up, output_weights, own_keys, own_values, shared_keys, shared_values, cached_lengths, prompt_group, slot_pages, padding_mask):
    flat_weights = input_weights.reshape(D_IN, 3 * HEADS * HD)
    flat_up = adapter_up.reshape(3, RANK, HEADS * HD).astype(jnp.float32)
    flat_out = output_weights.reshape(HEADS * HD, D)

    def one_request(request_items):
        hidden_rows, embed_rows, keys_own, values_own, length, group_index, pages, padding = request_items
        normed = normalize(hidden_rows, embed_rows, norm_gain)
        low_rank = to_narrow(jnp.dot(normed, adapter_down, preferred_element_type=jnp.float32))
        base_terms = jnp.dot(normed, flat_weights, preferred_element_type=jnp.float32).reshape(NEW, 3, HEADS * HD)
        lifted = jnp.einsum('ipr,prc->ipc', low_rank.reshape(NEW, 3, RANK).astype(jnp.float32), flat_up)
        projected = to_narrow(base_terms + lifted)
        queries = projected[:, 0].reshape(NEW, HEADS, HD)
        keys_new = projected[:, 1].reshape(NEW, HEADS, HD)
        values_new = projected[:, 2].reshape(NEW, HEADS, HD)
        positions = jnp.repeat(pages, PAGE, total_repeat_length=OWN_MAX) * PAGE + jnp.arange(OWN_MAX, dtype=jnp.int32) % PAGE
        own_usable = positions < length
        shared_k = lax.dynamic_index_in_dim(shared_keys, group_index, 0, keepdims=False)
        shared_v = lax.dynamic_index_in_dim(shared_values, group_index, 0, keepdims=False)

        def one_shard(shard_items):
            keys_part, values_part, usable_part, shared_kpart, shared_vpart = shard_items
            keys_all = jnp.concatenate([keys_part, shared_kpart], axis=0).reshape(-1, HEADS, HD)
            values_all = jnp.concatenate([values_part, shared_vpart], axis=0).reshape(-1, HEADS, HD)
            usable = jnp.concatenate([usable_part, jnp.ones((SHARED_DEV,), dtype=jnp.bool_)])[None, :]
            return block_partial(queries, keys_all, values_all, usable)
        shard_outputs, shard_peaks, shard_totals = lax.map(one_shard, (keys_own.reshape(N_SEQ, OWN_DEV, HEADS * HD), values_own.reshape(N_SEQ, OWN_DEV, HEADS * HD), own_usable.reshape(N_SEQ, OWN_DEV), shared_k.reshape(N_SEQ, SHARED_DEV, HEADS * HD), shared_v.reshape(N_SEQ, SHARED_DEV, HEADS * HD)))
        places = jnp.arange(NEW, dtype=jnp.int32)
        causal = places[:, None] >= places[None, :]
        new_output, new_peak, new_total = block_partial(queries, keys_new, values_new, causal)
        outputs = jnp.concatenate([shard_outputs, new_output[None]], axis=0).astype(jnp.float32)
        peak_scores = jnp.concatenate([shard_peaks, new_peak[None]], axis=0)
        totals = jnp.concatenate([shard_totals, new_total[None]], axis=0)
        attended = to_narrow(fold_partials(outputs, peak_scores, totals)).reshape(NEW, HEADS * HD)
        product = jnp.dot(attended, flat_out, preferred_element_type=jnp.float32)
        return (padding.astype(jnp.float32)[:, None] * product).astype(jnp.bfloat16)
    result = lax.map(one_request, (hidden_states.reshape(REQS, NEW, D), embeddings.reshape(REQS, NEW, D), own_keys, own_values, cached_lengths, prompt_group, slot_pages, padding_mask.reshape(REQS, NEW)))
    return result.reshape(TOKENS, D)
```

```python
import functools
import math

import jax
import jax.numpy as jnp
from jax import lax
from jax.experimental import pallas as pl
from jax.experimental.pallas import tpu as pltpu
from jax.sharding import PartitionSpec as P

HD = 128
PAGE = 64
MESH = pl.DeviceIdType.MESH
F32 = jnp.float32
BF16 = jnp.bfloat16

eps = 1e-05
neg_fill = -1e30


def normalize(hidden_states, embeddings, norm_gain):
    joined = jnp.concatenate([hidden_states, embeddings], axis=1).astype(jnp.float32)
    factor = lax.rsqrt(jnp.mean(joined * joined, axis=1, keepdims=True) + eps)
    return (joined * factor * norm_gain).astype(jnp.bfloat16)


def remote(src, dst, send, recv, target):
    return pltpu.make_async_remote_copy(
        src_ref=src, dst_ref=dst, send_sem=send, recv_sem=recv,
        device_id=target, device_id_type=MESH,
    )


def attend_tile(queries, keys, values, bias, scale):
    scores = lax.dot_general(queries, keys, (((1,), (1,)), ((), ())), preferred_element_type=F32)
    scores = scores + bias
    peak = jnp.max(scores, axis=1, keepdims=True)
    weights = jnp.exp2((scores - peak) * scale).astype(BF16)
    wide = jnp.concatenate([values, jnp.ones_like(values)], axis=1)
    both = jnp.dot(weights, wide, preferred_element_type=F32)
    total = both[:, HD:]
    return (both[:, :HD] / total).astype(BF16), peak * scale + jnp.log2(total)


def attention_kernel(
    length_ref, group_ref, pages_ref, q_ref, nk_ref, nv_ref, ok_ref, ov_ref, sk_ref, sv_ref,
    out_ref,
    kbuf, vbuf, skst, svst, bias, qbuf, osend, lsend, orecv, lrecv, orelay, lnew, onew,
    kv_loc, kv_snd, kv_rcv, sh_loc, sh_snd, sh_rcv, q_snd, q_rcv, o_snd, o_rcv, l_snd, l_rcv,
):
    seq_i, core = lax.axis_index("seq"), lax.rem(lax.axis_index("seq"), 2)
    zh = seq_i // 2
    places = kbuf.shape[0]
    own_count, shared_count = ok_ref.shape[1], sk_ref.shape[1]
    tokens, wide = q_ref.shape
    n_seq = 2 * places
    half = tokens // 2
    tile = min(128, half)
    scale = math.log2(math.e) / math.sqrt(HD)
    partner = {"seq": seq_i + 1 - 2 * core}
    above_i, below_i, far_i = (lax.rem(zh + k, places) for k in (1, places - 1, 2))
    above, below, far = ({"seq": 2 * i + core} for i in (above_i, below_i, far_i))

    barrier = pltpu.get_barrier_semaphore()
    for target in (partner, above, below, far):
        pl.semaphore_signal(barrier, inc=1, device_id=target, device_id_type=MESH)
    pl.semaphore_wait(barrier, 4)

    q_up = remote(q_ref, qbuf.at[zh], q_snd.at[0], q_rcv.at[0], above)
    q_down = remote(q_ref, qbuf.at[zh], q_snd.at[1], q_rcv.at[1], below)
    q_up.start()
    q_down.start()

    local, out_going = [], []
    for kv, (source, buffer) in enumerate(((ok_ref, kbuf), (ov_ref, vbuf))):
        for j in range(places):
            mine = pl.ds(pl.multiple_of((2 * j + core) * wide, wide), wide)
            other = pl.ds(pl.multiple_of((2 * j + 1 - core) * wide, wide), wide)
            local.append(pltpu.make_async_copy(
                source.at[0, :, mine], buffer.at[j, pl.ds(0, own_count), :], kv_loc.at[kv, j]))
            out_going.append(remote(
                source.at[0, :, other], buffer.at[j, pl.ds(own_count, own_count), :],
                kv_snd.at[kv, j], kv_rcv.at[kv, j], partner))
    for kv, (source, buffer) in enumerate(((sk_ref, skst), (sv_ref, svst))):
        for j in range(places):
            mine = pl.ds(pl.multiple_of((2 * j + core) * wide, wide), wide)
            other = pl.ds(pl.multiple_of((2 * j + 1 - core) * wide, wide), wide)
            local.append(pltpu.make_async_copy(
                source.at[:, :, mine], buffer.at[0, j], sh_loc.at[kv, j]))
            out_going.append(remote(
                source.at[:, :, other], buffer.at[1, j],
                sh_snd.at[kv, j], sh_rcv.at[kv, j], partner))
    for copy in local + out_going:
        copy.start()

    keys_in_all = bias.shape[1]
    pages_here = pages_ref.shape[1]
    page_count = pages_here * n_seq
    first = pages_ref[0, 0]
    first_other = lax.rem(first + page_count + pages_here * (1 - 2 * core), page_count)
    spots = lax.broadcasted_iota(jnp.int32, bias.shape, 1)
    limit_own = length_ref[0] - first * PAGE
    limit_other = length_ref[0] - first_other * PAGE + own_count
    usable = (spots >= 2 * own_count) | (spots < jnp.where(spots < own_count, limit_own, limit_other))
    bias[...] = jnp.where(usable, 0.0, neg_fill)

    qbuf[zh] = q_ref[...]

    def new_tile(t, carry):
        rows = pl.ds(pl.multiple_of(t * tile, tile), tile)
        row_ids = t * tile + lax.broadcasted_iota(jnp.int32, (tile, tokens), 0)
        col_ids = lax.broadcasted_iota(jnp.int32, (tile, tokens), 1)
        masked = jnp.where(col_ids <= row_ids, 0.0, neg_fill)
        for l in range(wide // HD):
            lanes = slice(l * HD, (l + 1) * HD)
            o, lse = attend_tile(q_ref[rows, lanes], nk_ref[:, lanes], nv_ref[:, lanes], masked, scale)
            onew[rows, lanes] = o
            lnew[l, rows, :] = lse
        return carry

    lax.fori_loop(0, tokens // tile, new_tile, 0)

    q_up.wait_recv()
    relay_up = remote(
        qbuf.at[below_i, pl.ds(0, half), :], qbuf.at[below_i, pl.ds(0, half), :],
        q_snd.at[2], q_rcv.at[2], above)
    relay_up.start()
    q_down.wait_recv()
    relay_down = remote(
        qbuf.at[above_i, pl.ds(half, half), :], qbuf.at[above_i, pl.ds(half, half), :],
        q_snd.at[3], q_rcv.at[3], below)
    relay_down.start()

    for copy in local:
        copy.wait()
    for copy in out_going:
        copy.wait()
    group = group_ref[0]
    for w in range(2):
        spot = pl.ds(2 * own_count + w * shared_count, shared_count)
        for j in range(places):
            kbuf[j, spot, :] = skst[w, j, group]
            vbuf[j, spot, :] = svst[w, j, group]

    def block(j, start, count, o_ref, l_ref):
        def one(t, carry):
            rows = pl.ds(pl.multiple_of(start + t * tile, tile), tile)
            lses = []
            for l in range(wide // HD):
                lanes = slice(l * HD, (l + 1) * HD)
                o, lse = attend_tile(
                    qbuf[j, rows, lanes], kbuf[j, :, lanes], vbuf[j, :, lanes], bias[0:1, :], scale)
                o_ref[j, rows, lanes] = o
                lses.append(lse)
            lane = lax.broadcasted_iota(jnp.int32, (tile, HD), 1)
            turned = jnp.where(lane < HD // 2, lses[0], lses[1]).T
            l_ref[j, 0:1, rows] = turned[0:1]
            l_ref[j, 1:2, rows] = turned[HD // 2:HD // 2 + 1]
            return carry

        lax.fori_loop(0, count // tile, one, 0)

    lsend[...] = jnp.zeros_like(lsend)
    block(zh, 0, tokens, orecv, lrecv)
    sends = []

    def give(j, target, k):
        o = remote(osend.at[j], orecv.at[zh], o_snd.at[k], o_rcv.at[k], target)
        l = remote(lsend.at[j], lrecv.at[zh], l_snd.at[k], l_rcv.at[k], target)
        o.start()
        l.start()
        sends.extend((o, l))

    block(below_i, 0, tokens, osend, lsend)
    give(below_i, below, 0)
    block(above_i, 0, tokens, osend, lsend)
    give(above_i, above, 1)

    relay_up.wait_recv()
    block(far_i, 0, half, osend, lsend)
    out_up = remote(osend.at[far_i, pl.ds(0, half), :], orelay.at[0], o_snd.at[2], o_rcv.at[2], above)
    out_up.start()
    relay_down.wait_recv()
    block(far_i, half, half, osend, lsend)
    out_down = remote(osend.at[far_i, pl.ds(half, half), :], orelay.at[1], o_snd.at[3], o_rcv.at[3], below)
    out_down.start()
    l_far = remote(lsend.at[far_i], lrecv.at[zh], l_snd.at[2], l_rcv.at[2], far)
    l_far.start()

    out_up.wait_recv()
    pass_up = remote(orelay.at[0], orecv.at[below_i, pl.ds(0, half), :], o_snd.at[4], o_rcv.at[4], above)
    pass_up.start()
    out_down.wait_recv()
    pass_down = remote(orelay.at[1], orecv.at[above_i, pl.ds(half, half), :], o_snd.at[5], o_rcv.at[5], below)
    pass_down.start()

    for copy in sends:
        copy.wait_recv()
    l_far.wait_recv()
    pass_up.wait_recv()
    pass_down.wait_recv()

    def merge(t, carry):
        rows = pl.ds(pl.multiple_of(t * tile, tile), tile)
        stats = [lrecv[b, :, rows] for b in range(places)]
        stats.append(jnp.zeros((HD - 8 * places, tile), F32))
        columns = jnp.concatenate(stats, axis=0).T
        for l in range(wide // HD):
            lanes = slice(l * HD, (l + 1) * HD)
            lses = [jnp.broadcast_to(columns[:, 8 * b + l:8 * b + l + 1], (tile, HD)) for b in range(places)]
            lses.append(lnew[l, rows, :])
            highest = functools.reduce(jnp.maximum, lses)
            parts = [orecv[b, rows, lanes] for b in range(places)] + [onew[rows, lanes]]
            weights = [jnp.exp2(x - highest) for x in lses]
            summed = functools.reduce(jnp.add, [w * p.astype(F32) for w, p in zip(weights, parts)])
            out_ref[rows, lanes] = (summed / functools.reduce(jnp.add, weights)).astype(BF16)
        return carry

    lax.fori_loop(0, tokens // tile, merge, 0)

    for copy in (q_up, q_down, relay_up, relay_down, out_up, out_down, l_far, pass_up, pass_down):
        copy.wait_send()
    for copy in sends:
        copy.wait_send()


def attention(cached_lengths, prompt_group, slot_pages, q, nk, nv, own_keys, own_values, shared_keys, shared_values):
    tokens, wide = q.shape
    places = own_keys.shape[2] // wide // 2
    own_count, shared_count = own_keys.shape[1], shared_keys.shape[1]
    groups = shared_keys.shape[0]
    keys_in_all = 2 * (own_count + shared_count)
    half = tokens // 2
    heads = wide // HD
    smem = pl.BlockSpec(memory_space=pltpu.SMEM)
    vmem = pl.BlockSpec(memory_space=pltpu.VMEM)
    hbm = pl.BlockSpec(memory_space=pl.ANY)
    dma = pltpu.SemaphoreType.DMA
    return pl.pallas_call(
        attention_kernel,
        out_shape=jax.ShapeDtypeStruct((tokens, wide), BF16),
        in_specs=[smem] * 3 + [vmem] * 3 + [hbm] * 4,
        out_specs=vmem,
        scratch_shapes=[
            pltpu.VMEM((places, keys_in_all, wide), BF16),
            pltpu.VMEM((places, keys_in_all, wide), BF16),
            pltpu.VMEM((2, places, groups, shared_count, wide), BF16),
            pltpu.VMEM((2, places, groups, shared_count, wide), BF16),
            pltpu.VMEM((8, keys_in_all), F32),
            pltpu.VMEM((places, tokens, wide), BF16),
            pltpu.VMEM((places, tokens, wide), BF16),
            pltpu.VMEM((places, 8, tokens), F32),
            pltpu.VMEM((places, tokens, wide), BF16),
            pltpu.VMEM((places, 8, tokens), F32),
            pltpu.VMEM((2, half, wide), BF16),
            pltpu.VMEM((heads, tokens, HD), F32),
            pltpu.VMEM((tokens, wide), BF16),
            dma((2, places)), dma((2, places)), dma((2, places)),
            dma((2, places)), dma((2, places)), dma((2, places)),
            dma((4,)), dma((4,)), dma((6,)), dma((6,)), dma((3,)), dma((3,)),
        ],
        compiler_params=pltpu.CompilerParams(
            collective_id=0, has_side_effects=True, vmem_limit_bytes=60 * 2**20),
    )(cached_lengths, prompt_group, slot_pages, q, nk, nv, own_keys, own_values, shared_keys, shared_values)


def shards(
    hidden_states,
    embeddings,
    norm_gain,
    input_weights,
    adapter_down,
    adapter_up,
    output_weights,
    own_keys,
    own_values,
    shared_keys,
    shared_values,
    cached_lengths,
    prompt_group,
    slot_pages,
    padding_mask,
):
    normed = normalize(hidden_states, embeddings, norm_gain)
    gathered = lax.all_gather(normed, "seq", axis=0, tiled=True)
    new_count = gathered.shape[0]
    low_sum = jnp.dot(
        gathered,
        lax.all_gather(adapter_down, ("seq", "mp"), axis=0, tiled=True),
        preferred_element_type=jnp.float32,
    )
    low_rank = low_sum.astype(jnp.bfloat16)
    width = input_weights.shape[3]
    piece = lax.all_gather(input_weights, "dp", axis=0, tiled=True)
    base_terms = jnp.dot(
        gathered, piece.reshape(piece.shape[0], 3 * width), preferred_element_type=jnp.float32
    )
    rank_size = adapter_up.shape[1]
    lifted = jnp.einsum(
        "ipr,prc->ipc",
        low_rank.reshape(new_count, 3, rank_size),
        adapter_up[:, :, 0, :],
        preferred_element_type=jnp.float32,
    )
    projected = (base_terms.reshape(new_count, 3, width) + lifted).astype(jnp.bfloat16)
    attended = attention(
        cached_lengths, prompt_group, slot_pages,
        projected[:, 0], projected[:, 1], projected[:, 2],
        own_keys, own_values, shared_keys, shared_values)
    out_matrix = lax.all_gather(output_weights, "dp", axis=2, tiled=True)[0]
    summed = lax.psum_scatter(
        jnp.dot(attended, out_matrix, preferred_element_type=jnp.float32).astype(jnp.bfloat16),
        ("seq", "mp"),
        scatter_dimension=0,
        tiled=True,
    ).astype(jnp.float32)
    return (padding_mask.astype(jnp.float32)[:, None] * summed).astype(jnp.bfloat16)


def solution(mesh):
    placed = (
        P(("dp", "seq"), None),
        P(("dp", "seq"), None),
        P(),
        P("dp", None, "mp", "seq"),
        P(("seq", "mp"), None),
        P(None, None, "mp", "seq"),
        P("mp", "seq", "dp"),
        P("dp", "seq", "mp"),
        P("dp", "seq", "mp"),
        P(None, "seq", "mp"),
        P(None, "seq", "mp"),
        P("dp"),
        P("dp"),
        P("dp", "seq"),
        P(("dp", "seq", "mp")),
    )
    return jax.shard_map(
        shards, mesh=mesh, in_specs=placed, out_specs=P(("dp", "seq", "mp"), None), check_vma=False
    )
```
